32 devices in a mesh: dom: 2 (over x), pair: 8 (over z, y), aux: 2 (over core).
Axes of the slice: x: 2, y: 2, z: 4, core: 2. Of those that a mesh axis runs over, the one named last changes fastest.
Arguments:
- three_index: bfloat16 [3072, 16, 512], P('aux', ('dom', 'pair')), parts along dimension 1, may hold values from -0.796875 to 0.796875
- metric: bfloat16 [6144, 3072], P(('dom', 'pair'), 'aux'), parts along dimension 0, as said below
- occ_energy: float32 [16], P('dom'), parts along dimension 0, may hold values from -2 to -0.4
- vir_energy: float32 [1024], P('dom'), parts along dimension 0, may hold values from 0.2 to 3
- pair_list: int32 [16, 3, 2], P('dom'), parts along dimension 0, may hold values from -1 to 7, as said below
Outputs:
- density: float32 [3072, 16, 512], P('aux', ('dom', 'pair')), parts along dimension 1
The draws below stay inside these ranges and needn't reach their ends.
There are 2 independent parts, one for each index of `dom`. The reference program is written for one: setup_inputs(seed, part) draws one part's arguments, and reference() takes and returns one part's arrays. A program takes and returns all parts, laid end to end along the dimension named above; each array names one. Nothing has to cross between parts.
Inputs may be any that keep to these rules, and one draw needn't show every extreme that they name: metric is symmetric up to rounding. `pair_list`: row b lists pairs (b, (b + d) mod 8) for distinct d of 1 to 3, in any order of slots; unused slots hold -1 in both columns; every row lists at least one pair, and some row lists 3.
All inputs are finite; a program needn't handle non-finite values.
Results may differ from the reference program's by a relative error of at most 0.0034.
Values may be sent and summed in bfloat16 or wider, within the bound.
No kernel may reach another device: no remote copies, remote signals or barrier semaphores. Data moves between devices by JAX's collectives and lax.ppermute only.
A program may use at most 128 MiB of HBM per device.

```python
import jax
import jax.numpy as jnp
from jax import lax

NAUX = 3072
V = 512
OCC_DEV = 1
DMAX = 3
OCC = 8
N_PAIR = 8


def draw_metric(key, part):
    noise = jax.random.normal(jax.random.fold_in(key, 5), (NAUX, NAUX), jnp.float32) * NAUX ** (-0.5)
    matrix = 0.5 * (noise + noise.T) + jnp.eye(NAUX, dtype=jnp.float32)
    return matrix.astype(jnp.bfloat16)


def draw_pair_list(key, part):
    row_keys = jax.random.split(jax.random.fold_in(key, 11), N_PAIR)

    def one_row(row_key, row_block):
        category = jax.random.randint(jax.random.fold_in(row_key, 1), (), 0, 4)
        listed_count = jnp.where(category == 0, DMAX, jnp.where(category == 1, min(2, DMAX), 1))
        listed_count = jnp.where(row_block == 0, DMAX, listed_count)
        shifts = jax.random.permutation(jax.random.fold_in(row_key, 2), DMAX) + 1
        in_use = jnp.arange(DMAX) < listed_count
        partner = (row_block + shifts) % N_PAIR
        left_block = jnp.where(in_use, row_block, -1)
        second = jnp.where(in_use, partner, -1)
        return jnp.stack([left_block, second], axis=-1).astype(jnp.int32)
    return jax.vmap(one_row)(row_keys, jnp.arange(N_PAIR, dtype=jnp.int32))


def block_levels(own_key, extent, pieces, least, high):
    factor_of, own = 1.0, jax.random.fold_in(own_key, 6)
    for dim, parts in pieces:
        heights = jnp.exp(jax.random.uniform(jax.random.fold_in(own, dim), (parts,), jnp.float32, least / len(pieces), high / len(pieces)))
        factor_of = factor_of * jnp.repeat(heights, extent[dim] // parts).reshape([-1 if axis == dim else 1 for axis in range(len(extent))])
    return factor_of


def bell_draw(key, shape, spread, limit, shards=(), kind=jnp.bfloat16):
    values = spread * jax.random.normal(key, shape, jnp.float32)
    if shards:
        values = values * block_levels(key, shape, shards, -0.22, 0.18)
    return jnp.clip(values, -limit, limit).astype(kind)


def setup_inputs(seed: int = 0, part: int = 0) -> dict:
    streams_of = jax.random.split(jax.random.key(seed), 6)
    part_keys = jax.random.split(jax.random.fold_in(streams_of[5], part), 6)
    return {
        "three_index": bell_draw(part_keys[0], (NAUX, OCC, V), 0.13, 0.796875, ((0, 2), (1, 8))),
        "metric": draw_metric(jax.random.fold_in(jax.random.fold_in(streams_of[5], part), 71), part),
        "occ_energy": jnp.clip(jax.random.uniform(part_keys[2], (OCC,), jnp.float32, -2.0, -0.4), -2.0, -0.4),
        "vir_energy": jnp.clip(jax.random.uniform(part_keys[3], (V,), jnp.float32, 0.2, 3.0), 0.2, 3.0),
        "pair_list": draw_pair_list(jax.random.fold_in(jax.random.fold_in(streams_of[5], part), 71), part),
    }


def reference(three_index, metric, occ_energy, vir_energy, pair_list):
    naux_rows, occ_rows, virtuals = three_index.shape
    flattened = three_index.reshape(naux_rows, occ_rows * virtuals)
    fitted = jnp.dot(metric, flattened, preferred_element_type=jnp.float32).astype(jnp.bfloat16)
    coeffs = fitted.astype(jnp.float32).reshape(naux_rows, N_PAIR, OCC_DEV, virtuals)
    occ_blocks = occ_energy.reshape(N_PAIR, OCC_DEV)
    block_ids = jnp.arange(N_PAIR, dtype=jnp.int32)
    density = jnp.zeros((naux_rows, N_PAIR, OCC_DEV, virtuals), jnp.float32)
    for offset in range(DMAX + 1):
        partner_ids = (block_ids + offset) % N_PAIR
        if offset == 0:
            active = jnp.ones((N_PAIR,), jnp.float32)
        else:
            active = jnp.any(pair_list[:, :, 1] == partner_ids[:, None], axis=1).astype(jnp.float32)
        right_side = jnp.roll(coeffs, -offset, axis=1)
        right_energy = jnp.roll(occ_blocks, -offset, axis=0)
        integrals = jnp.einsum("qpia,qpjb->pijab", coeffs, right_side)
        denominator = (occ_blocks[:, :, None, None, None] + right_energy[:, None, :, None, None]
                       - vir_energy[None, None, None, :, None] - vir_energy[None, None, None, None, :])
        amplitude = integrals / denominator
        mixed = (2.0 * amplitude - jnp.swapaxes(amplitude, 3, 4)) * active[:, None, None, None, None]
        mixed = mixed.astype(jnp.bfloat16).astype(jnp.float32)
        density = density + jnp.einsum("pijab,qpjb->qpia", mixed, right_side)
        if offset > 0:
            partner = jnp.einsum("pijab,qpia->qpjb", mixed, coeffs).astype(jnp.bfloat16)
            partner = lax.optimization_barrier(partner).astype(jnp.float32)
            density = density + jnp.roll(partner, offset, axis=1)
    return density.reshape(naux_rows, occ_rows, virtuals)
```

```python
import jax
import jax.numpy as jnp
from jax import lax
from jax.sharding import PartitionSpec as P


def shifted(block, axis, distance):
    devices = range(lax.axis_size(axis))
    route = [((i - distance) % len(devices), i) for i in devices]
    return lax.ppermute(block, axis, route)


def swap_aux(x):
    return lax.ppermute(x, "aux", [(0, 1), (1, 0)])


def dot(x, y, cx, cy):
    return lax.dot_general(x, y, (((cx,), (cy,)), ((), ())), preferred_element_type=jnp.float32)


def ladder(orbital_block, metric, occ_energy, vir_energy, pair_list):
    slab_rows, _, virtuals = orbital_block.shape
    t_own = orbital_block.reshape(slab_rows, virtuals)
    count = lax.axis_size("pair")
    b = lax.axis_index("pair")
    core = lax.axis_index("aux")
    rung = b // 2
    inner = (rung == 1) | (rung == 2)
    right = (rung >= 2).astype(jnp.int32)
    rows = metric.shape[0]

    def send(x, route):
        return lax.ppermute(x, "pair", route)

    side_swap = [(p, p ^ 1) for p in range(count)]
    rung_swap = [(p, p ^ 2) for p in range(count)]
    mid = [(2, 4), (3, 5), (4, 2), (5, 3)]
    outward = [(2, 0), (3, 1), (4, 6), (5, 7)]

    def cores(route, which):
        return [(2 * s + which(s), 2 * d + which(s)) for s, d in route]

    def diag_core(p):
        return 0 if p < count // 2 else 1

    def far_core(p):
        return 1 - diag_core(p)

    def send_core(x, route, which):
        return lax.ppermute(x, ("pair", "aux"), cores(route, which))

    t_other = swap_aux(t_own)

    m_y = send(metric, side_swap)
    m_z = send(metric, rung_swap)
    far3i = send_core(metric, mid, diag_core)
    half = rows // 2
    far3o = send_core(far3i, outward, far_core)
    far4i = send_core(m_z, mid, diag_core)
    m_yz_top = send(m_z[:half], side_swap)
    m_yz_bot = send(m_y[half:], rung_swap)
    far4o = send_core(far4i, outward, far_core)
    far3 = jnp.where(inner, far3i, far3o)
    far4 = jnp.where(inner, far4i, far4o)
    far_swap = [(p, p ^ 1) for p in range(count)]
    far3y = send_core(far3, far_swap, far_core)
    far4y = send_core(far4, far_swap, far_core)
    m_yz = jnp.concatenate([m_yz_top, m_yz_bot], 0)

    near = [metric, m_y, m_z, m_yz]
    side = b % 2
    low = rung % 2

    def ordered(own, y, z, yz):
        e0 = jnp.where(side == 0, own, y)
        e1 = jnp.where(side == 0, y, own)
        g0 = jnp.where(side == 0, z, yz)
        g1 = jnp.where(side == 0, yz, z)
        return jnp.concatenate(
            [
                jnp.where(low == 0, e0, g0),
                jnp.where(low == 0, e1, g1),
                jnp.where(low == 0, g0, e0),
                jnp.where(low == 0, g1, e1),
            ],
            0,
        )

    block = ordered(*near)
    f3a = jnp.where(side == 0, far3, far3y)
    f3b = jnp.where(side == 0, far3y, far3)
    f4a = jnp.where(side == 0, far4, far4y)
    f4b = jnp.where(side == 0, far4y, far4)
    far_block = jnp.where(
        right == 0,
        jnp.concatenate([f3a, f3b, f4a, f4b], 0),
        jnp.concatenate([f4a, f4b, f3a, f3b], 0),
    )
    aux_route = [(2 * p + far_core(p), 2 * p + diag_core(p)) for p in range(count)]
    off_from = lax.ppermute(block, ("pair", "aux"), aux_route)
    on_diag = core == right
    diag = jnp.where(on_diag, block, far_block)
    off = jnp.where(on_diag, off_from, block)
    fitted = dot(diag, t_own, 0, 0) + lax.cond(
        on_diag, lambda o, t: dot(o, t, 1, 0), lambda o, t: dot(o, t, 0, 0), off, t_other
    )
    f = fitted.astype(jnp.bfloat16)

    f_y = send(f, side_swap)
    v2 = send(f, rung_swap)
    v3i = send(f, mid)
    v2_y = send(v2, side_swap)
    v3o = send(v3i, outward)
    v4i = send(v2, mid)
    v3 = jnp.where(inner, v3i, v3o)
    v3_y = send(v3, side_swap)
    v4o = send(v4i, outward)
    v4 = jnp.where(inner, v4i, v4o)
    v4_y = send(v4, side_swap)

    near_rung = rung ^ 1
    in_other = jnp.where(right == 0, 2, 1)
    out_other = jnp.where(right == 0, 3, 0)
    work = [
        (f, b),
        (f_y, b ^ 1),
        (v2, 2 * near_rung + side),
        (v2_y, 2 * near_rung + 1 - side),
        (v3, 2 * in_other + side),
        (v3_y, 2 * in_other + 1 - side),
        (v4, 2 * out_other + side),
        (v4_y, 2 * out_other + 1 - side),
    ]
    second = pair_list[:, :, 1]
    own_list = second[b]
    own_energy = occ_energy[b]
    vir_sum = vir_energy[:, None] + vir_energy[None, :]
    density = jnp.zeros((slab_rows, virtuals), jnp.float32)
    for g, j in work:
        partial = dot(f, g, 0, 0)
        total = partial + swap_aux(partial)
        amplitude = total / (own_energy + occ_energy[j] - vir_sum)
        listed = (j == b) | jnp.any(own_list == j) | jnp.any(second[j] == b)
        mixed = jnp.where(listed, 2.0 * amplitude - amplitude.T, 0.0).astype(jnp.bfloat16)
        density = density + dot(g, mixed, 1, 1)
    return density.reshape(slab_rows, 1, virtuals)


def pair_product(left_side, right_side):
    return jnp.einsum("qia,qjb->ijab", left_side, right_side, preferred_element_type=jnp.float32)


def ring(three_index, metric, occ_energy, vir_energy, pair_list):
    slab_rows, orbitals, virtuals = three_index.shape
    flattened = three_index.reshape(slab_rows, orbitals * virtuals)
    stacked = lax.all_gather(flattened, "aux", axis=0, tiled=True)
    metric_half = lax.all_gather(metric, "pair", axis=0, tiled=True)
    fitted = dot(metric_half, stacked, 0, 0)
    coeffs = fitted.astype(jnp.bfloat16).reshape(slab_rows, orbitals, virtuals)
    pair_count = lax.axis_size("pair")
    my_block = lax.axis_index("pair")
    farthest = pair_list.shape[1]
    listed = lax.dynamic_index_in_dim(pair_list, my_block, 0, keepdims=False)[:, 1]
    own_energy = lax.dynamic_slice_in_dim(occ_energy, my_block * orbitals, orbitals)
    density = jnp.zeros((slab_rows, orbitals, virtuals), jnp.float32)
    for offset in range(farthest + 1):
        target = (my_block + offset) % pair_count
        partner = shifted(coeffs, "pair", -offset) if offset else coeffs
        energy = lax.dynamic_slice_in_dim(occ_energy, target * orbitals, orbitals)
        active = jnp.any(listed == target) | (offset == 0)
        partial = pair_product(coeffs, partner)
        summed = lax.psum(partial, "aux")
        amplitude = summed / (
            own_energy[:, None, None, None]
            + energy[None, :, None, None]
            - vir_energy[None, None, :, None]
            - vir_energy[None, None, None, :]
        )
        mixed = jnp.where(active, 2.0 * amplitude - jnp.swapaxes(amplitude, 2, 3), 0.0)
        mixed = mixed.astype(jnp.bfloat16)
        density = density + jnp.einsum(
            "ijab,qjb->qia", mixed, partner, preferred_element_type=jnp.float32
        )
        if offset:
            term = jnp.einsum("ijab,qia->qjb", mixed, coeffs, preferred_element_type=jnp.float32)
            arrived = shifted(term.astype(jnp.bfloat16), "pair", offset)
            density = density + arrived.astype(jnp.float32)
    return density


def solution(mesh):
    def local(three_index, metric, occ_energy, vir_energy, pair_list):
        rungs = mesh.shape["pair"] // 2
        small = rungs == 4 and mesh.shape["aux"] == 2 and three_index.shape[1] == 1
        plan = ladder if small else ring
        return plan(three_index, metric, occ_energy, vir_energy, pair_list)

    return jax.shard_map(
        local,
        mesh=mesh,
        in_specs=(
            P("aux", ("dom", "pair"), None),
            P(("dom", "pair"), "aux"),
            P("dom"),
            P("dom"),
            P("dom", None, None),
        ),
        out_specs=P("aux", ("dom", "pair"), None),
        check_vma=False,
    )
```
